128 devices in a mesh: narrow: 4 (over y_hi, core), wide: 32 (over z, y_lo, x).
Axes of the slice: x: 4, y: 4 (y_hi: 2, y_lo: 2; y = y_hi * 2 + y_lo), z: 4, core: 2. Of those that a mesh axis runs over, the one named last changes fastest.
Arguments:
- residual: float32 [16, 2048, 2048], P(None, 'wide', 'narrow'), may hold values from -6 to 6
- counts: int32 [16, 2048, 2048], P(None, 'wide', 'narrow'), may hold values from 0 to 4
- screening: float32 [16], replicated, may hold values from 0.02 to 0.5
- even_y: float32 [1024, 1024], replicated, may hold values from -0.1875 to 0.1875
- odd_y: float32 [1024, 1024], replicated, may hold values from -0.1875 to 0.1875
- even_z: float32 [1024, 1024], replicated, may hold values from -0.1875 to 0.1875
- odd_z: float32 [1024, 1024], replicated, may hold values from -0.1875 to 0.1875
- lam_y: float32 [2048], replicated, may hold values from 0.05 to 4
- lam_z: float32 [2048], replicated, may hold values from 0.05 to 4
Outputs:
- correction: float32 [16, 2048, 2048], P(None, 'wide', 'narrow')
The draws below stay inside these ranges and needn't reach their ends.
All inputs are finite; a program needn't handle non-finite values.
Results may differ from the reference program's by a relative error of at most 0.000071.
Values sent between devices are 32-bit elements; how exact they have to be, the bound alone decides.
No kernel may reach another device: no remote copies, remote signals or barrier semaphores. Data moves between devices by JAX's collectives and lax.ppermute only.
A program may use at most 192 MiB of HBM per device.

```python
import math
import jax
import jax.numpy as jnp
from jax import lax

NY = 2048
NZ = 2048
PLANES = 16


def touch_ends(entries, stream_key, least, largest):
    spot = [jax.random.randint(jax.random.fold_in(stream_key, axis), (), 0, length) for axis, length in enumerate(entries.shape)]
    main_axis = entries.shape.index(max(entries.shape))
    beside = spot[:main_axis] + [(spot[main_axis] + 1) % entries.shape[main_axis]] + spot[main_axis + 1:]
    return entries.at[tuple(spot)].set(least).at[tuple(beside)].set(largest)


def block_levels(rng, extent, split, least, top_value):
    loudness = 1.0
    for position, shards_of in split:
        draws = jax.random.uniform(jax.random.fold_in(jax.random.fold_in(rng, 6), position), (shards_of,), jnp.float32, least / len(split), top_value / len(split))
        loudness = loudness * jnp.repeat(jnp.exp(draws), extent[position] // shards_of).reshape((-1,) + (1,) * (len(extent) - 1 - position))
    return loudness


def noise(rng, dims, spread, reach, shards=(), held_as=jnp.bfloat16):
    array = jax.random.normal(rng, dims, jnp.float32) * spread
    if len(shards) > 0:
        array = block_levels(rng, dims, shards, -0.22, 0.18) * array
    return jnp.clip(array, min=-reach, max=reach).astype(held_as)


def setup_inputs(seed: int = 0) -> dict:
    key_list = jax.random.split(jax.random.key(seed), 10)
    residual = noise(key_list[0], (PLANES, NZ, NY), 1.0, 6.0, ((1, 32), (2, 4)), jnp.float32)
    counts = touch_ends(jax.random.randint(key_list[1], (PLANES, NZ, NY), 0, 5), jax.random.fold_in(key_list[1], 1), 0, 4).astype(jnp.int32)
    screening = jnp.clip(jnp.exp(jax.random.uniform(key_list[2], (PLANES,), jnp.float32, math.log(0.02), math.log(0.5))), 0.02, 0.5)
    even_y = noise(key_list[3], (NY // 2, NY // 2), (NY // 2) ** -0.5, 0.1875, (), jnp.float32)
    odd_y = noise(key_list[4], (NY // 2, NY // 2), (NY // 2) ** -0.5, 0.1875, (), jnp.float32)
    even_z = noise(key_list[5], (NZ // 2, NZ // 2), (NZ // 2) ** -0.5, 0.1875, (), jnp.float32)
    odd_z = noise(key_list[6], (NZ // 2, NZ // 2), (NZ // 2) ** -0.5, 0.1875, (), jnp.float32)
    lam_y = jnp.clip(jnp.exp(jax.random.uniform(key_list[7], (NY,), jnp.float32, math.log(0.05), math.log(4.0))), 0.05, 4.0)
    lam_z = jnp.clip(jnp.exp(jax.random.uniform(key_list[8], (NZ,), jnp.float32, math.log(0.05), math.log(4.0))), 0.05, 4.0)
    return dict(residual=residual, counts=counts, screening=screening, even_y=even_y, odd_y=odd_y, even_z=even_z, odd_z=odd_z, lam_y=lam_y, lam_z=lam_z)


def matmul(left, right):
    return jnp.dot(left, right, preferred_element_type=jnp.float32, precision=lax.Precision.HIGHEST)


def reference(residual, counts, screening, even_y, odd_y, even_z, odd_z, lam_y, lam_z):
    half_y = NY // 2
    half_z = NZ // 2

    def plane_solve(item):
        plane_res, plane_counts, shift = item
        source = plane_res + 0.3 * (plane_counts.astype(jnp.float32) - 2.0)
        flipped = source[:, ::-1]
        along = jnp.concatenate([matmul(source[:, :half_y] + flipped[:, :half_y], even_y),
                                 matmul(source[:, :half_y] - flipped[:, :half_y], odd_y)], 1)
        flipped = along[::-1]
        spectral = jnp.concatenate([matmul(even_z.T, along[:half_z] + flipped[:half_z]),
                                    matmul(odd_z.T, along[:half_z] - flipped[:half_z])], 0)
        scaled = spectral / (lam_z[:, None] + lam_y[None, :] + shift)
        zeven = matmul(even_z, scaled[:half_z])
        zodd = matmul(odd_z, scaled[half_z:])
        back = jnp.concatenate([zeven + zodd, (zeven - zodd)[::-1]], 0)
        yeven = matmul(back[:, :half_y], even_y.T)
        yodd = matmul(back[:, half_y:], odd_y.T)
        return jnp.concatenate([yeven + yodd, (yeven - yodd)[:, ::-1]], 1)

    return lax.map(plane_solve, (residual, counts, screening))
```

```python
import jax
import jax.numpy as jnp
from jax import lax
from jax.experimental import pallas as pl
from jax.experimental.pallas import tpu as pltpu
from jax.sharding import Mesh, PartitionSpec as P

F32 = jnp.float32
BF16 = jnp.bfloat16
ROWS = 256
TILE = 256
HALF = 1024
GATHER_Y = ("yh", "z", "yl", "core")
GATHER_Z = ("x", "core")
VMEM = pl.BlockSpec(memory_space=pltpu.VMEM)
NN = (((1,), (0,)), ((), ()))
NT = (((1,), (1,)), ((), ()))
TN = (((0,), (0,)), ((), ()))


def split(value):
    high = value.astype(BF16)
    low = (value - high.astype(F32)).astype(BF16)
    return high, low


def dot(left, right, dims):
    return lax.dot_general(left, right, dims, preferred_element_type=F32)


def product(left, right, dims):
    return (
        dot(left[0], right[0], dims)
        + dot(left[0], right[1], dims)
        + dot(left[1], right[0], dims)
    )


def mirror():
    row = lax.broadcasted_iota(jnp.int32, (TILE, TILE), 0)
    column = lax.broadcasted_iota(jnp.int32, (TILE, TILE), 1)
    return jnp.where(row + column == TILE - 1, 1.0, 0.0).astype(BF16)


def flip_lanes(value, flipper):
    high, low = split(value)
    return dot(high, flipper, NN) + dot(low, flipper, NN)


def flip_rows(value, flipper):
    high, low = split(value)
    return dot(flipper, high, NN) + dot(flipper, low, NN)


def split_kernel(matrix_ref, high_ref, low_ref):
    high_ref[...], low_ref[...] = split(matrix_ref[...])


def split_matrix(matrix):
    block = pl.BlockSpec((256, HALF), lambda i: (i, 0))
    return pl.pallas_call(
        split_kernel,
        grid=(HALF // 256,),
        in_specs=[block],
        out_specs=[block, block],
        out_shape=[jax.ShapeDtypeStruct((HALF, HALF), BF16)] * 2,
        name="split_matrix",
    )(matrix)


def forward_y_kernel(x_ref, eh_ref, el_ref, oh_ref, ol_ref, out_ref):
    flipper = mirror()
    sym, anti = [], []
    for core in range(2):
        for part in range(2):
            lanes = slice(part * TILE, (part + 1) * TILE)
            other = slice((1 - part) * TILE, (2 - part) * TILE)
            low = x_ref[0, :, core, :, lanes].reshape(ROWS, TILE)
            high = x_ref[1, :, 1 - core, :, other].reshape(ROWS, TILE)
            high = flip_lanes(high, flipper)
            sym.append(split(low + high))
            anti.append(split(low - high))
    for base, sides, h_ref, l_ref in ((0, sym, eh_ref, el_ref), (4, anti, oh_ref, ol_ref)):
        left = tuple(jnp.concatenate([s[i] for s in sides], 1) for i in range(2))
        for block in range(4):
            lanes = slice(block * TILE, (block + 1) * TILE)
            out_ref[base + block] = product(left, (h_ref[:, lanes], l_ref[:, lanes]), NN)


def forward_y(x, even, odd):
    return pl.pallas_call(
        forward_y_kernel,
        in_specs=[VMEM] * 5,
        out_specs=VMEM,
        out_shape=jax.ShapeDtypeStruct((8, ROWS, TILE), F32),
        compiler_params=pltpu.CompilerParams(vmem_limit_bytes=48 << 20),
        name="forward_y",
    )(x.reshape(2, 8, 2, 32, 512), *even, *odd)


def solve_z_kernel(x_ref, eh_ref, el_ref, oh_ref, ol_ref, lam_ref, shift_ref, out_ref):
    flipper = mirror()
    sym, anti = [], []
    for t in range(4):
        low = x_ref[:, t].reshape(TILE, TILE)
        high = flip_rows(x_ref[:, 7 - t].reshape(TILE, TILE), flipper)
        sym.append(split(low + high))
        anti.append(split(low - high))
    results = []
    for parity, sides, h_ref, l_ref in ((0, sym, eh_ref, el_ref), (1, anti, oh_ref, ol_ref)):
        right = tuple(jnp.concatenate([s[i] for s in sides], 0) for i in range(2))
        matrix = (h_ref[...], l_ref[...])
        spectral = product(matrix, right, TN)
        scaled = spectral / (lam_ref[parity] + shift_ref[...])
        results.append(product(matrix, split(scaled), NN))
    total = results[0] + results[1]
    rest = results[0] - results[1]
    for t in range(4):
        rows = slice(t * TILE, (t + 1) * TILE)
        out_ref[:, t] = total[rows].reshape(8, 32, TILE)
        out_ref[:, 7 - t] = flip_rows(rest[rows], flipper).reshape(8, 32, TILE)


def solve_z(x, even, odd, lam, shift):
    return pl.pallas_call(
        solve_z_kernel,
        in_specs=[VMEM] * 7,
        out_specs=VMEM,
        out_shape=jax.ShapeDtypeStruct((8, 8, 32, TILE), F32),
        compiler_params=pltpu.CompilerParams(vmem_limit_bytes=48 << 20),
        name="solve_z",
    )(x.reshape(8, 8, 32, TILE), *even, *odd, lam, shift)


def backward_y_kernel(x_ref, eh_ref, el_ref, oh_ref, ol_ref, out_ref):
    flipper = mirror()
    even = split(jnp.concatenate([x_ref[i] for i in range(4)], 1))
    odd = split(jnp.concatenate([x_ref[i] for i in range(4, 8)], 1))
    for block in range(4):
        core, part = divmod(block, 2)
        rows = slice(block * TILE, (block + 1) * TILE)
        yeven = product(even, (eh_ref[rows], el_ref[rows]), NT)
        yodd = product(odd, (oh_ref[rows], ol_ref[rows]), NT)
        lanes = slice(part * TILE, (part + 1) * TILE)
        other = slice((1 - part) * TILE, (2 - part) * TILE)
        out_ref[0, :, core, :, lanes] = (yeven + yodd).reshape(8, 32, TILE)
        flipped = flip_lanes(yeven - yodd, flipper)
        out_ref[1, :, 1 - core, :, other] = flipped.reshape(8, 32, TILE)


def backward_y(x, even, odd):
    return pl.pallas_call(
        backward_y_kernel,
        in_specs=[VMEM] * 5,
        out_specs=VMEM,
        out_shape=jax.ShapeDtypeStruct((2, 8, 2, 32, 512), F32),
        compiler_params=pltpu.CompilerParams(vmem_limit_bytes=48 << 20),
        name="backward_y",
    )(x, *even, *odd)


def on_device(residual, counts, screening, even_y, odd_y, even_z, odd_z, lam_y, lam_z):
    plane = (lax.axis_index("yh") * 4 + lax.axis_index("z")) * 2 + lax.axis_index("yl")
    modes = lax.axis_index("x") * 2 + lax.axis_index("core")
    source = residual + 0.3 * (counts.astype(F32) - 2.0)
    gathered = lax.all_to_all(source.reshape(32, 32, 512), GATHER_Y, 0, 0, tiled=True)
    ey, oy, ez, oz = (split_matrix(m) for m in (even_y, odd_y, even_z, odd_z))
    shift = lax.dynamic_slice_in_dim(lam_y, modes * TILE, TILE)
    shift = (shift + lax.dynamic_slice_in_dim(screening, plane, 1)).reshape(1, TILE)
    lam = lam_z.reshape(2, HALF, 1)
    along = forward_y(gathered, ey, oy)
    columns = lax.all_to_all(along, GATHER_Z, 0, 0, tiled=True)
    back = solve_z(columns, ez, oz, lam, shift)
    rows = lax.all_to_all(back.reshape(8, ROWS, TILE), GATHER_Z, 0, 0, tiled=True)
    done = backward_y(rows, ey, oy)
    done = lax.all_to_all(done.reshape(32, 32, 512), GATHER_Y, 0, 0, tiled=True)
    return done.reshape(16, 64, 512)


def solution(mesh):
    fine = Mesh(mesh.devices.reshape(2, 2, 4, 2, 4), ("yh", "core", "z", "yl", "x"))
    split_spec = P(None, ("z", "yl", "x"), ("yh", "core"))
    return jax.shard_map(
        on_device,
        mesh=fine,
        in_specs=(split_spec, split_spec) + (P(),) * 7,
        out_specs=split_spec,
        check_vma=False,
    )
```

```python
import jax
import jax.numpy as jnp
from jax import lax
from jax.experimental import pallas as pl
from jax.experimental.pallas import tpu as pltpu
from jax.sharding import Mesh, PartitionSpec as P

F32 = jnp.float32
BF16 = jnp.bfloat16
TILE = 256
LANES = 128
HALF = 1024
ROWS = 256
SOURCE_LIMIT = 52
PREPARE_LIMIT = 8
KERNEL_LIMIT = 12
NARROW = ("yh", "core")
WIDE = ("z", "yl", "x")
VMEM = pl.BlockSpec(memory_space=pltpu.VMEM)
HBM = pl.BlockSpec(memory_space=pltpu.HBM)
NN = (((1,), (0,)), ((), ()))
NT = (((1,), (1,)), ((), ()))
TN = (((0,), (0,)), ((), ()))


def split(value):
    high = value.astype(BF16)
    low = (value - high.astype(F32)).astype(BF16)
    return high, low


def dot(left, right, dims):
    return lax.dot_general(left, right, dims, preferred_element_type=F32)


def product(left, right, dims):
    return (
        dot(left[0], right[0], dims)
        + dot(left[0], right[1], dims)
        + dot(left[1], right[0], dims)
    )


def mirror():
    row = lax.broadcasted_iota(jnp.int32, (TILE, TILE), 0)
    column = lax.broadcasted_iota(jnp.int32, (TILE, TILE), 1)
    return jnp.where(row + column == TILE - 1, 1.0, 0.0).astype(BF16)


def flip_lanes(value, flipper):
    high, low = split(value)
    return dot(high, flipper, NN) + dot(low, flipper, NN)


def flip_rows(value, flipper):
    high, low = split(value)
    return dot(flipper, high, NN) + dot(flipper, low, NN)


def low_quarter(across):
    core, yh = lax.axis_index("core"), lax.axis_index("yh")
    return jnp.bitwise_xor(jnp.bitwise_xor(core, yh), across)


def call(kernel, name, in_specs, out_specs, out_shape, scratch, limit, flops, **more):
    return pl.pallas_call(
        kernel,
        in_specs=in_specs,
        out_specs=out_specs,
        out_shape=out_shape,
        scratch_shapes=scratch,
        compiler_params=pltpu.CompilerParams(vmem_limit_bytes=limit << 20),
        cost_estimate=pl.CostEstimate(flops=flops, transcendentals=0, bytes_accessed=10 << 20),
        name=name,
        **more,
    )


def source_kernel(order, residual, counts, *refs):
    outs, residual_buffer, counts_buffer, sems = refs[:-3], *refs[-3:]
    me = lax.axis_index(NARROW)
    steps = [(i, part) for i in range(len(order)) for part in range(2)]

    def copies(step):
        i, part = step
        planes = pl.ds(4 * jnp.bitwise_xor(me, order[i]) + 2 * part, 2)
        slot = 2 * i + part
        yield pltpu.make_async_copy(residual.at[planes], residual_buffer.at[slot], sems.at[0, slot])
        yield pltpu.make_async_copy(counts.at[planes], counts_buffer.at[slot], sems.at[1, slot])

    for step in steps:
        for copy in copies(step):
            copy.start()
    for step in steps:
        for copy in copies(step):
            copy.wait()
        i, part = step
        slot = 2 * i + part
        value = residual_buffer[slot] + 0.3 * (counts_buffer[slot].astype(F32) - 2.0)
        outs[i][part * 128 : (part + 1) * 128] = value.reshape(128, 512)


def make_source(order, residual, counts):
    def kernel(*refs):
        source_kernel(order, *refs)

    count = len(order)
    return call(
        kernel,
        "make_source",
        [HBM] * 2,
        [VMEM] * count,
        [jax.ShapeDtypeStruct((ROWS, 512), F32)] * count,
        [
            pltpu.VMEM((2 * count, 2, 64, 512), F32),
            pltpu.VMEM((2 * count, 2, 64, 512), jnp.int32),
            pltpu.SemaphoreType.DMA((2, 2 * count)),
        ],
        SOURCE_LIMIT,
        1 << 20,
    )(residual, counts)


def prepare_kernel(*refs):
    matrices, outs, buffer, sems = refs[:4], refs[4:12], *refs[12:]
    steps = [(m, r) for m in range(4) for r in range(4)]

    def fetch(index):
        matrix, rows = steps[index]
        source = matrices[matrix].at[pl.ds(rows * TILE, TILE)]
        return pltpu.make_async_copy(source, buffer.at[index % 4], sems.at[index % 4])

    for index in range(3):
        fetch(index).start()
    for index, (matrix, rows) in enumerate(steps):
        if index + 3 < 16:
            fetch(index + 3).start()
        fetch(index).wait()
        high, low = split(buffer[index % 4])
        outs[2 * matrix][rows * TILE : (rows + 1) * TILE] = high
        outs[2 * matrix + 1][rows * TILE : (rows + 1) * TILE] = low


def prepare(*matrices):
    outs = call(
        prepare_kernel,
        "prepare",
        [HBM] * 4,
        [VMEM] * 8,
        [jax.ShapeDtypeStruct((HALF, HALF), BF16)] * 8,
        [pltpu.VMEM((4, TILE, HALF), F32), pltpu.SemaphoreType.DMA((4,))],
        PREPARE_LIMIT,
        4 << 30,
    )(*matrices)
    return outs[:4], outs[4:]


def send(block, d):
    return lax.ppermute(block, NARROW, [(n, n ^ d) for n in range(4)])


def forward_y_kernel(across, near_ref, far_ref, eh, el, oh, ol, *refs):
    held, out_ref, halves = refs[:-2], refs[-2], refs[-1]
    yh = lax.axis_index("yh")
    halves[yh] = near_ref[...]
    halves[1 - yh] = far_ref[...]
    flipper = mirror()
    sym, anti = [], []
    for part in range(2):
        low = halves[0, :, part * TILE : (part + 1) * TILE]
        high = flip_lanes(halves[1, :, (1 - part) * TILE : (2 - part) * TILE], flipper)
        sym.append(split(low + high))
        anti.append(split(low - high))
    rows = pl.ds(pl.multiple_of(512 * low_quarter(across), 512), 512)
    for base, sides, high, low in ((0, sym, eh, el), (4, anti, oh, ol)):
        left = tuple(jnp.concatenate([s[i] for s in sides], 1) for i in range(2))
        for block in range(4):
            lanes = slice(block * TILE, (block + 1) * TILE)
            result = product(left, (high[rows, lanes], low[rows, lanes]), NN)
            result = result.reshape(4, 64, TILE)
            if held:
                result = result + held[0][:, base + block]
            out_ref[:, base + block] = result


def forward_y(across, near, far, matrices, held):
    def kernel(*refs):
        forward_y_kernel(across, *refs)

    more = [] if held is None else [held]
    return call(
        kernel,
        "forward_y",
        [VMEM] * (6 + len(more)),
        VMEM,
        jax.ShapeDtypeStruct((4, 8, 64, TILE), F32),
        [pltpu.VMEM((2, ROWS, 512), F32)],
        KERNEL_LIMIT,
        2 << 30,
    )(near, far, *matrices, *more)


def pieces(value):
    high = value.astype(BF16)
    rest = value - high.astype(F32)
    middle = rest.astype(BF16)
    low = (rest - middle.astype(F32)).astype(BF16)
    return [high.astype(F32), middle.astype(F32), low.astype(F32)]


def solve_z_kernel(x_ref, eh, el, oh, ol, lamz_ref, lamy_ref, screen_ref, out_ref):
    flipper = mirror()
    place = lax.axis_index(WIDE)
    plane, modes = 4 * lax.axis_index(NARROW) + place // 8, place % 8
    shift = jnp.concatenate([lamy_ref[pl.ds(2 * modes + i, 1)] for i in range(2)], 1)
    shift = pieces(shift + screen_ref[plane])
    shift = jnp.concatenate(shift + [jnp.ones((1, TILE), F32)] * 3, 0).astype(BF16)
    sym, anti = [], []
    for block in range(4):
        low = x_ref[4 * block : 4 * block + 4].reshape(TILE, TILE)
        high = x_ref[28 - 4 * block : 32 - 4 * block].reshape(TILE, TILE)
        high = flip_rows(high, flipper)
        sym.append(split(low + high))
        anti.append(split(low - high))
    results = []
    for parity, sides, matrix in ((0, sym, (eh, el)), (1, anti, (oh, ol))):
        right = tuple(jnp.concatenate([s[i] for s in sides], 0) for i in range(2))
        pair = (matrix[0][...], matrix[1][...])
        spectral = product(pair, right, TN)
        lam = jnp.concatenate([lamz_ref[8 * parity + i : 8 * parity + i + 1] for i in range(8)], 1)
        lam = jnp.concatenate([jnp.ones((1, HALF), F32)] * 3 + pieces(lam), 0).astype(BF16)
        scaled = spectral / dot(lam, shift, TN)
        results.append(product(pair, split(scaled), NN))
    total = results[0] + results[1]
    rest = results[0] - results[1]
    for block in range(4):
        rows = slice(block * TILE, (block + 1) * TILE)
        out_ref[4 * block : 4 * block + 4] = total[rows].reshape(4, 64, TILE)
        flipped = flip_rows(rest[rows], flipper)
        out_ref[28 - 4 * block : 32 - 4 * block] = flipped.reshape(4, 64, TILE)


def solve_z(x, matrices, lam_z, lam_y, screening):
    return call(
        solve_z_kernel,
        "solve_z",
        [VMEM] * 7 + [pl.BlockSpec(memory_space=pltpu.SMEM)],
        VMEM,
        jax.ShapeDtypeStruct((32, 64, TILE), F32),
        [],
        KERNEL_LIMIT,
        6 << 30,
    )(x, *matrices, lam_z.reshape(16, LANES), lam_y.reshape(16, LANES), screening)


def backward_y_kernel(across, x_ref, eh, el, oh, ol, near_ref, far_ref, halves):
    flipper = mirror()
    sides = []
    for parity in range(2):
        blocks = [x_ref[:, 4 * parity + i].reshape(ROWS, TILE) for i in range(4)]
        sides.append(split(jnp.concatenate(blocks, 1)))
    start = 512 * low_quarter(across)
    for part in range(2):
        rows = pl.ds(pl.multiple_of(start + part * TILE, TILE), TILE)
        even = product(sides[0], (eh[rows], el[rows]), NT)
        odd = product(sides[1], (oh[rows], ol[rows]), NT)
        halves[0, :, part * TILE : (part + 1) * TILE] = even + odd
        flipped = flip_lanes(even - odd, flipper)
        halves[1, :, (1 - part) * TILE : (2 - part) * TILE] = flipped
    yh = lax.axis_index("yh")
    near_ref[...] = halves[yh]
    far_ref[...] = halves[1 - yh]


def backward_y(across, x, matrices):
    def kernel(*refs):
        backward_y_kernel(across, *refs)

    return call(
        kernel,
        "backward_y",
        [VMEM] * 5,
        [VMEM] * 2,
        [jax.ShapeDtypeStruct((ROWS, 512), F32)] * 2,
        [pltpu.VMEM((2, ROWS, 512), F32)],
        KERNEL_LIMIT,
        2 << 30,
    )(x, *matrices)


def place_kernel(order, *refs):
    blocks, out, sems = refs[: len(order)], refs[-2], refs[-1]
    me = lax.axis_index(NARROW)
    steps = [(i, part) for i in range(len(order)) for part in range(2)]

    def copy(i, part):
        start = ROWS * jnp.bitwise_xor(me, order[i]) + part * 128
        target = out.at[pl.ds(pl.multiple_of(start, 128), 128)]
        source = blocks[i].at[pl.ds(part * 128, 128)]
        return pltpu.make_async_copy(source, target, sems.at[i, part])

    for step in steps:
        copy(*step).start()
    for step in steps:
        copy(*step).wait()


def place(order, blocks, held):
    def kernel(*refs):
        place_kernel(order, *refs)

    more = [] if held is None else [held]
    return call(
        kernel,
        "place",
        [pl.BlockSpec(memory_space=pl.ANY)] * len(order) + [HBM] * len(more),
        HBM,
        jax.ShapeDtypeStruct((HALF, 512), F32),
        [pltpu.SemaphoreType.DMA((len(order), 2))],
        2,
        1 << 20,
        input_output_aliases={} if held is None else {len(order): 0},
    )(*blocks, *more)


def on_device(residual, counts, screening, even_y, odd_y, even_z, odd_z, lam_y, lam_z):
    (block2,) = make_source((2,), residual, counts)
    block3, block1, block0 = make_source((3, 1, 0), residual, counts)
    block2, block3, block1 = send(block2, 2), send(block3, 3), send(block1, 1)
    matrix_y, matrix_z = prepare(even_y, odd_y, even_z, odd_z)
    along = forward_y(1, block1, block2, matrix_y, None)
    along = forward_y(0, block0, block3, matrix_y, along)
    columns = lax.all_to_all(along.reshape(32, 64, TILE), WIDE, 0, 0, tiled=True)
    back = solve_z(columns, matrix_z, lam_z, lam_y, screening)
    rows = lax.all_to_all(back, WIDE, 0, 0, tiled=True).reshape(4, 8, 64, TILE)
    block1, block2 = backward_y(1, rows, matrix_y)
    block0, block3 = backward_y(0, rows, matrix_y)
    block2, block3, block1 = send(block2, 2), send(block3, 3), send(block1, 1)
    out = place((0, 1, 2), (block0, block1, block2), None)
    out = place((3,), (block3,), out)
    return out.reshape(16, 64, 512)


def solution(mesh):
    fine = Mesh(mesh.devices.reshape(2, 2, 4, 2, 4), ("yh", "core", "z", "yl", "x"))
    split_spec = P(None, WIDE, NARROW)
    return jax.shard_map(
        on_device,
        mesh=fine,
        in_specs=(split_spec, split_spec) + (P(),) * 7,
        out_specs=split_spec,
        check_vma=False,
    )
```

```python
import jax
import jax.numpy as jnp
from jax import lax
from jax.experimental import pallas as pl
from jax.experimental.pallas import tpu as pltpu
from jax.sharding import Mesh, PartitionSpec as P

F32 = jnp.float32
BF16 = jnp.bfloat16
TILE = 256
LANES = 128
HALF = 1024
ROWS = 256
SOURCE_LIMIT = 52
PREPARE_LIMIT = 8
KERNEL_LIMIT = 12
NARROW = ("yh", "core")
WIDE = ("z", "yl", "x")
VMEM = pl.BlockSpec(memory_space=pltpu.VMEM)
HBM = pl.BlockSpec(memory_space=pltpu.HBM)
NN = (((1,), (0,)), ((), ()))
NT = (((1,), (1,)), ((), ()))
TN = (((0,), (0,)), ((), ()))


def split(value):
    high = value.astype(BF16)
    low = (value - high.astype(F32)).astype(BF16)
    return high, low


def dot(left, right, dims):
    return lax.dot_general(left, right, dims, preferred_element_type=F32)


def product(left, right, dims):
    return (
        dot(left[0], right[0], dims)
        + dot(left[0], right[1], dims)
        + dot(left[1], right[0], dims)
    )


def mirror():
    row = lax.broadcasted_iota(jnp.int32, (TILE, TILE), 0)
    column = lax.broadcasted_iota(jnp.int32, (TILE, TILE), 1)
    return jnp.where(row + column == TILE - 1, 1.0, 0.0).astype(BF16)


def flip_lanes(value, flipper):
    high, low = split(value)
    return dot(high, flipper, NN) + dot(low, flipper, NN)


def flip_rows(value, flipper):
    high, low = split(value)
    return dot(flipper, high, NN) + dot(flipper, low, NN)


def low_quarter(across):
    core, yh = lax.axis_index("core"), lax.axis_index("yh")
    return jnp.bitwise_xor(jnp.bitwise_xor(core, yh), across)


def call(kernel, name, in_specs, out_specs, out_shape, scratch, limit, flops, **more):
    return pl.pallas_call(
        kernel,
        in_specs=in_specs,
        out_specs=out_specs,
        out_shape=out_shape,
        scratch_shapes=scratch,
        compiler_params=pltpu.CompilerParams(vmem_limit_bytes=limit << 20),
        cost_estimate=pl.CostEstimate(flops=flops, transcendentals=0, bytes_accessed=10 << 20),
        name=name,
        **more,
    )


def source_kernel(order, residual, counts, *refs):
    outs, residual_buffer, counts_buffer, sems = refs[:-3], *refs[-3:]
    me = lax.axis_index(NARROW)
    steps = [(i, part) for i in range(len(order)) for part in range(2)]

    def copies(step):
        i, part = step
        planes = pl.ds(4 * jnp.bitwise_xor(me, order[i]) + 2 * part, 2)
        slot = 2 * i + part
        yield pltpu.make_async_copy(residual.at[planes], residual_buffer.at[slot], sems.at[0, slot])
        yield pltpu.make_async_copy(counts.at[planes], counts_buffer.at[slot], sems.at[1, slot])

    for step in steps:
        for copy in copies(step):
            copy.start()
    for step in steps:
        for copy in copies(step):
            copy.wait()
        i, part = step
        slot = 2 * i + part
        value = residual_buffer[slot] + 0.3 * (counts_buffer[slot].astype(F32) - 2.0)
        outs[i][part * 128 : (part + 1) * 128] = value.reshape(128, 512)


def make_source(order, residual, counts):
    def kernel(*refs):
        source_kernel(order, *refs)

    count = len(order)
    return call(
        kernel,
        "make_source",
        [HBM] * 2,
        [VMEM] * count,
        [jax.ShapeDtypeStruct((ROWS, 512), F32)] * count,
        [
            pltpu.VMEM((2 * count, 2, 64, 512), F32),
            pltpu.VMEM((2 * count, 2, 64, 512), jnp.int32),
            pltpu.SemaphoreType.DMA((2, 2 * count)),
        ],
        SOURCE_LIMIT,
        1 << 20,
    )(residual, counts)


def prepare_kernel(*refs):
    matrices, outs, buffer, sems = refs[:2], refs[2:6], *refs[6:]
    steps = [(m, r) for m in range(2) for r in range(4)]

    def fetch(index):
        matrix, rows = steps[index]
        source = matrices[matrix].at[pl.ds(rows * TILE, TILE)]
        return pltpu.make_async_copy(source, buffer.at[index % 4], sems.at[index % 4])

    for index in range(3):
        fetch(index).start()
    for index, (matrix, rows) in enumerate(steps):
        if index + 3 < 8:
            fetch(index + 3).start()
        fetch(index).wait()
        high, low = split(buffer[index % 4])
        outs[2 * matrix][rows * TILE : (rows + 1) * TILE] = high
        outs[2 * matrix + 1][rows * TILE : (rows + 1) * TILE] = low


def prepare(*matrices):
    return call(
        prepare_kernel,
        "prepare",
        [HBM] * 2,
        [VMEM] * 4,
        [jax.ShapeDtypeStruct((HALF, HALF), BF16)] * 4,
        [pltpu.VMEM((4, TILE, HALF), F32), pltpu.SemaphoreType.DMA((4,))],
        PREPARE_LIMIT,
        2 << 30,
    )(*matrices)


def send(block, d, cores=(0, 1)):
    return lax.ppermute(block, NARROW, [(n, n ^ d) for n in range(4) if n % 2 in cores])


def forward_y_kernel(across, near_ref, far0_ref, far1_ref, eh, el, oh, ol, _, *refs):
    held, out_ref, halves = refs[:-2], refs[-2], refs[-1]
    yh = lax.axis_index("yh")
    halves[yh] = near_ref[...]
    for core, far_ref in enumerate((far0_ref, far1_ref)):

        @pl.when(lax.axis_index("core") == core)
        def _(far_ref=far_ref):
            halves[1 - yh] = far_ref[...]

    flipper = mirror()
    sym, anti = [], []
    for part in range(2):
        low = halves[0, :, part * TILE : (part + 1) * TILE]
        high = flip_lanes(halves[1, :, (1 - part) * TILE : (2 - part) * TILE], flipper)
        sym.append(split(low + high))
        anti.append(split(low - high))
    rows = pl.ds(pl.multiple_of(512 * low_quarter(across), 512), 512)
    for base, sides, high, low in ((0, sym, eh, el), (4, anti, oh, ol)):
        left = tuple(jnp.concatenate([s[i] for s in sides], 1) for i in range(2))
        for block in range(4):
            lanes = slice(block * TILE, (block + 1) * TILE)
            result = product(left, (high[rows, lanes], low[rows, lanes]), NN)
            result = result.reshape(4, 64, TILE)
            if held:
                result = result + held[0][:, base + block]
            out_ref[:, base + block] = result


def forward_y(across, near, far, matrices, token, held):
    def kernel(*refs):
        forward_y_kernel(across, *refs)

    more = [] if held is None else [held]
    return call(
        kernel,
        "forward_y",
        [VMEM] * (8 + len(more)),
        VMEM,
        jax.ShapeDtypeStruct((4, 8, 64, TILE), F32),
        [pltpu.VMEM((2, ROWS, 512), F32)],
        KERNEL_LIMIT,
        2 << 30,
    )(near, *far, *matrices, token, *more)


def pieces(value):
    high = value.astype(BF16)
    rest = value - high.astype(F32)
    middle = rest.astype(BF16)
    low = (rest - middle.astype(F32)).astype(BF16)
    return [high.astype(F32), middle.astype(F32), low.astype(F32)]


def solve_z_kernel(x_ref, eh, el, oh, ol, lamz_ref, lamy_ref, screen_ref, out_ref):
    flipper = mirror()
    place = lax.axis_index(WIDE)
    plane, modes = 4 * lax.axis_index(NARROW) + place // 8, place % 8
    shift = jnp.concatenate([lamy_ref[pl.ds(2 * modes + i, 1)] for i in range(2)], 1)
    shift = pieces(shift + screen_ref[plane])
    shift = jnp.concatenate(shift + [jnp.ones((1, TILE), F32)] * 3, 0).astype(BF16)
    sym, anti = [], []
    for block in range(4):
        low = x_ref[4 * block : 4 * block + 4].reshape(TILE, TILE)
        high = x_ref[28 - 4 * block : 32 - 4 * block].reshape(TILE, TILE)
        high = flip_rows(high, flipper)
        sym.append(split(low + high))
        anti.append(split(low - high))
    results = []
    for parity, sides, matrix in ((0, sym, (eh, el)), (1, anti, (oh, ol))):
        right = tuple(jnp.concatenate([s[i] for s in sides], 0) for i in range(2))
        pair = (matrix[0][...], matrix[1][...])
        spectral = product(pair, right, TN)
        lam = jnp.concatenate([lamz_ref[8 * parity + i : 8 * parity + i + 1] for i in range(8)], 1)
        lam = jnp.concatenate([jnp.ones((1, HALF), F32)] * 3 + pieces(lam), 0).astype(BF16)
        scaled = spectral / dot(lam, shift, TN)
        results.append(product(pair, split(scaled), NN))
    total = results[0] + results[1]
    rest = results[0] - results[1]
    for block in range(4):
        rows = slice(block * TILE, (block + 1) * TILE)
        out_ref[4 * block : 4 * block + 4] = total[rows].reshape(4, 64, TILE)
        flipped = flip_rows(rest[rows], flipper)
        out_ref[28 - 4 * block : 32 - 4 * block] = flipped.reshape(4, 64, TILE)


def solve_z(x, matrices, lam_z, lam_y, screening):
    return call(
        solve_z_kernel,
        "solve_z",
        [VMEM] * 7 + [pl.BlockSpec(memory_space=pltpu.SMEM)],
        VMEM,
        jax.ShapeDtypeStruct((32, 64, TILE), F32),
        [],
        KERNEL_LIMIT,
        6 << 30,
    )(x, *matrices, lam_z.reshape(16, LANES), lam_y.reshape(16, LANES), screening)


def backward_y_kernel(across, x_ref, eh, el, oh, ol, near_ref, far_ref, halves):
    flipper = mirror()
    sides = []
    for parity in range(2):
        blocks = [x_ref[:, 4 * parity + i].reshape(ROWS, TILE) for i in range(4)]
        sides.append(split(jnp.concatenate(blocks, 1)))
    start = 512 * low_quarter(across)
    for part in range(2):
        rows = pl.ds(pl.multiple_of(start + part * TILE, TILE), TILE)
        even = product(sides[0], (eh[rows], el[rows]), NT)
        odd = product(sides[1], (oh[rows], ol[rows]), NT)
        halves[0, :, part * TILE : (part + 1) * TILE] = even + odd
        flipped = flip_lanes(even - odd, flipper)
        halves[1, :, (1 - part) * TILE : (2 - part) * TILE] = flipped
    yh = lax.axis_index("yh")
    near_ref[...] = halves[yh]
    far_ref[...] = halves[1 - yh]


def backward_y(across, x, matrices):
    def kernel(*refs):
        backward_y_kernel(across, *refs)

    return call(
        kernel,
        "backward_y",
        [VMEM] * 5,
        [VMEM] * 2,
        [jax.ShapeDtypeStruct((ROWS, 512), F32)] * 2,
        [pltpu.VMEM((2, ROWS, 512), F32)],
        KERNEL_LIMIT,
        2 << 30,
    )(x, *matrices)


def place_kernel(order, *refs):
    blocks, out, sems = refs[: len(order)], refs[-2], refs[-1]
    me = lax.axis_index(NARROW)
    steps = [(i, part) for i in range(len(order)) for part in range(2)]

    def copy(i, part):
        start = ROWS * jnp.bitwise_xor(me, order[i]) + part * 128
        target = out.at[pl.ds(pl.multiple_of(start, 128), 128)]
        source = blocks[i].at[pl.ds(part * 128, 128)]
        return pltpu.make_async_copy(source, target, sems.at[i, part])

    for step in steps:
        copy(*step).start()
    for step in steps:
        copy(*step).wait()


def place(order, blocks, held):
    def kernel(*refs):
        place_kernel(order, *refs)

    more = [] if held is None else [held]
    return call(
        kernel,
        "place",
        [pl.BlockSpec(memory_space=pl.ANY)] * len(order) + [HBM] * len(more),
        HBM,
        jax.ShapeDtypeStruct((HALF, 512), F32),
        [pltpu.SemaphoreType.DMA((len(order), 2))],
        2,
        1 << 20,
        input_output_aliases={} if held is None else {len(order): 0},
    )(*blocks, *more)


def on_device(residual, counts, screening, even_y, odd_y, even_z, odd_z, lam_y, lam_z):
    block3, block2 = make_source((3, 2), residual, counts)
    block1, block0 = make_source((1, 0), residual, counts)
    block3, block1, block0 = lax.optimization_barrier((send(block3, 1), block1, block0))
    own0, sibling0 = send(block2, 2, (0,)), send(block3, 2, (0,))
    block1 = send(block1, 1)
    matrix_y, matrix_z = prepare(even_y, odd_y), prepare(even_z, odd_z)
    block1, sibling0, own0, matrix_y, matrix_z = lax.optimization_barrier(
        (block1, sibling0, own0, matrix_y, matrix_z)
    )
    token = send(sibling0[:8, :LANES], 1, (0,))
    block2, block3, token = lax.optimization_barrier((block2, block3, token))
    own1, sibling1 = send(block2, 2, (1,)), send(block3, 2, (1,))
    along = forward_y(1, block1, (own0, own1), matrix_y, token, None)
    along = forward_y(0, block0, (sibling0, sibling1), matrix_y, token, along)
    columns = lax.all_to_all(along.reshape(32, 64, TILE), WIDE, 0, 0, tiled=True)
    back = solve_z(columns, matrix_z, lam_z, lam_y, screening)
    rows = lax.all_to_all(back, WIDE, 0, 0, tiled=True).reshape(4, 8, 64, TILE)
    block1, block2 = backward_y(1, rows, matrix_y)
    block0, block3 = backward_y(0, rows, matrix_y)
    block2, block3 = send(block2, 2), send(block3, 2)
    block1, block2 = lax.optimization_barrier((block1, block2))
    block1, block3 = send(block1, 1), send(block3, 1)
    out = place((0, 1, 2), (block0, block1, block2), None)
    out = place((3,), (block3,), out)
    return out.reshape(16, 64, 512)


def solution(mesh):
    fine = Mesh(mesh.devices.reshape(2, 2, 4, 2, 4), ("yh", "core", "z", "yl", "x"))
    split_spec = P(None, WIDE, NARROW)
    return jax.shard_map(
        on_device,
        mesh=fine,
        in_specs=(split_spec, split_spec) + (P(),) * 7,
        out_specs=split_spec,
        check_vma=False,
    )
```

```python
import jax
import jax.numpy as jnp
from jax import lax
from jax.experimental import pallas as pl
from jax.experimental.pallas import tpu as pltpu
from jax.sharding import Mesh, PartitionSpec as P

F32 = jnp.float32
BF16 = jnp.bfloat16
TILE = 256
LANES = 128
HALF = 1024
ROWS = 256
SOURCE_LIMIT = 52
PREPARE_LIMIT = 8
KERNEL_LIMIT = 12
NARROW = ("yh", "core")
WIDE = ("z", "x")
PLACES = ("yh", "core", "yl")
VMEM = pl.BlockSpec(memory_space=pltpu.VMEM)
HBM = pl.BlockSpec(memory_space=pltpu.HBM)
NN = (((1,), (0,)), ((), ()))
NT = (((1,), (1,)), ((), ()))
TN = (((0,), (0,)), ((), ()))


def split(value):
    high = value.astype(BF16)
    low = (value - high.astype(F32)).astype(BF16)
    return high, low


def dot(left, right, dims):
    return lax.dot_general(left, right, dims, preferred_element_type=F32)


def product(left, right, dims):
    return (
        dot(left[0], right[0], dims)
        + dot(left[0], right[1], dims)
        + dot(left[1], right[0], dims)
    )


def mirror():
    row = lax.broadcasted_iota(jnp.int32, (TILE, TILE), 0)
    column = lax.broadcasted_iota(jnp.int32, (TILE, TILE), 1)
    return jnp.where(row + column == TILE - 1, 1.0, 0.0).astype(BF16)


def flip_lanes(value, flipper):
    high, low = split(value)
    return dot(high, flipper, NN) + dot(low, flipper, NN)


def flip_rows(value, flipper):
    high, low = split(value)
    return dot(flipper, high, NN) + dot(flipper, low, NN)


def low_quarter(across):
    core, yh = lax.axis_index("core"), lax.axis_index("yh")
    return jnp.bitwise_xor(jnp.bitwise_xor(core, yh), across)


def call(kernel, name, in_specs, out_specs, out_shape, scratch, limit, flops, **more):
    return pl.pallas_call(
        kernel,
        in_specs=in_specs,
        out_specs=out_specs,
        out_shape=out_shape,
        scratch_shapes=scratch,
        compiler_params=pltpu.CompilerParams(vmem_limit_bytes=limit << 20),
        cost_estimate=pl.CostEstimate(flops=flops, transcendentals=0, bytes_accessed=10 << 20),
        name=name,
        **more,
    )


def source_kernel(order, residual, counts, *refs):
    outs, residual_buffer, counts_buffer, sems = refs[:-3], *refs[-3:]
    me = lax.axis_index(NARROW)
    steps = [(i, part) for i in range(len(order)) for part in range(2)]

    def copies(step):
        i, part = step
        kept = jnp.bitwise_xor(lax.axis_index("yl"), part)
        planes = pl.ds(4 * jnp.bitwise_xor(me, order[i]) + 2 * kept, 2)
        slot = 2 * i + part
        yield pltpu.make_async_copy(residual.at[planes], residual_buffer.at[slot], sems.at[0, slot])
        yield pltpu.make_async_copy(counts.at[planes], counts_buffer.at[slot], sems.at[1, slot])

    for step in steps:
        for copy in copies(step):
            copy.start()
    for step in steps:
        for copy in copies(step):
            copy.wait()
        i, part = step
        slot = 2 * i + part
        value = residual_buffer[slot] + 0.3 * (counts_buffer[slot].astype(F32) - 2.0)
        outs[i][part * 128 : (part + 1) * 128] = value.reshape(128, 512)


def make_source(order, residual, counts):
    def kernel(*refs):
        source_kernel(order, *refs)

    count = len(order)
    return call(
        kernel,
        "make_source",
        [HBM] * 2,
        [VMEM] * count,
        [jax.ShapeDtypeStruct((ROWS, 512), F32)] * count,
        [
            pltpu.VMEM((2 * count, 2, 64, 512), F32),
            pltpu.VMEM((2 * count, 2, 64, 512), jnp.int32),
            pltpu.SemaphoreType.DMA((2, 2 * count)),
        ],
        SOURCE_LIMIT,
        1 << 20,
    )(residual, counts)


def prepare_kernel(*refs):
    matrices, outs, buffer, sems = refs[:2], refs[2:6], *refs[6:]
    steps = [(m, r) for m in range(2) for r in range(4)]

    def fetch(index):
        matrix, rows = steps[index]
        source = matrices[matrix].at[pl.ds(rows * TILE, TILE)]
        return pltpu.make_async_copy(source, buffer.at[index % 4], sems.at[index % 4])

    for index in range(3):
        fetch(index).start()
    for index, (matrix, rows) in enumerate(steps):
        if index + 3 < 8:
            fetch(index + 3).start()
        fetch(index).wait()
        high, low = split(buffer[index % 4])
        outs[2 * matrix][rows * TILE : (rows + 1) * TILE] = high
        outs[2 * matrix + 1][rows * TILE : (rows + 1) * TILE] = low


def prepare(*matrices):
    return call(
        prepare_kernel,
        "prepare",
        [HBM] * 2,
        [VMEM] * 4,
        [jax.ShapeDtypeStruct((HALF, HALF), BF16)] * 4,
        [pltpu.VMEM((4, TILE, HALF), F32), pltpu.SemaphoreType.DMA((4,))],
        PREPARE_LIMIT,
        2 << 30,
    )(*matrices)


def send(block, d, cores=(0, 1)):
    pairs = [(n, n ^ d) for n in range(8) if n // 2 % 2 in cores]
    return lax.ppermute(block, PLACES, pairs)


def forward_y_kernel(across, near_ref, first, second, eh, el, oh, ol, _, *refs):
    held, out_ref, halves = refs[:-2], refs[-2], refs[-1]
    yh, yl = lax.axis_index("yh"), lax.axis_index("yl")
    here, there = (pl.ds(pl.multiple_of(128 * v, 128), 128) for v in (yl, 1 - yl))
    near_rows = pl.ds(128 * across, 128)
    far_rows = pl.ds(128 * (1 - across), 128)
    halves[yh, here] = near_ref[0:128]
    for core, ways in enumerate((first, second)):

        @pl.when(lax.axis_index("core") == core)
        def _(ways=ways):
            halves[yh, there] = ways[0][near_rows]
            halves[1 - yh, here] = ways[1][far_rows]
            halves[1 - yh, there] = ways[2][far_rows]

    flipper = mirror()
    sym, anti = [], []
    for part in range(2):
        low = halves[0, :, part * TILE : (part + 1) * TILE]
        high = flip_lanes(halves[1, :, (1 - part) * TILE : (2 - part) * TILE], flipper)
        sym.append(split(low + high))
        anti.append(split(low - high))
    rows = pl.ds(pl.multiple_of(512 * low_quarter(across), 512), 512)
    for base, sides, high, low in ((0, sym, eh, el), (4, anti, oh, ol)):
        left = tuple(jnp.concatenate([s[i] for s in sides], 1) for i in range(2))
        for block in range(4):
            lanes = slice(block * TILE, (block + 1) * TILE)
            result = product(left, (high[rows, lanes], low[rows, lanes]), NN)
            for half in range(2):
                for plane in range(2):
                    start = 128 * half + 64 * plane
                    piece = result[start : start + 64]
                    if held:
                        piece = piece + held[0][plane, base + block, half]
                    out_ref[plane, base + block, half] = piece


def forward_y(across, near, first, second, matrices, token, held):
    def kernel(near_ref, *refs):
        forward_y_kernel(across, near_ref, refs[:3], refs[3:6], *refs[6:])

    more = [] if held is None else [held]
    return call(
        kernel,
        "forward_y",
        [VMEM] * (12 + len(more)),
        VMEM,
        jax.ShapeDtypeStruct((2, 8, 2, 64, TILE), F32),
        [pltpu.VMEM((2, ROWS, 512), F32)],
        KERNEL_LIMIT,
        2 << 30,
    )(near, *first, *second, *matrices, token, *more)


def pieces(value):
    high = value.astype(BF16)
    rest = value - high.astype(F32)
    middle = rest.astype(BF16)
    low = (rest - middle.astype(F32)).astype(BF16)
    return [high.astype(F32), middle.astype(F32), low.astype(F32)]


def inverse_kernel(lamz_ref, lamy_ref, screen_ref, out_ref):
    place = lax.axis_index(WIDE)
    plane = 4 * lax.axis_index(NARROW) + 2 * lax.axis_index("yl") + place // 8
    modes = place % 8
    shift = jnp.concatenate([lamy_ref[pl.ds(2 * modes + i, 1)] for i in range(2)], 1)
    shift = pieces(shift + screen_ref[plane])
    shift = jnp.concatenate(shift + [jnp.ones((1, TILE), F32)] * 3, 0).astype(BF16)
    for parity in range(2):
        lam = jnp.concatenate([lamz_ref[8 * parity + i : 8 * parity + i + 1] for i in range(8)], 1)
        lam = jnp.concatenate([jnp.ones((1, HALF), F32)] * 3 + pieces(lam), 0).astype(BF16)
        out_ref[parity] = 1.0 / dot(lam, shift, TN)


def inverse(lam_z, lam_y, screening):
    return call(
        inverse_kernel,
        "inverse",
        [VMEM] * 2 + [pl.BlockSpec(memory_space=pltpu.SMEM)],
        VMEM,
        jax.ShapeDtypeStruct((2, HALF, TILE), F32),
        [],
        8,
        1 << 30,
    )(lam_z.reshape(16, LANES), lam_y.reshape(16, LANES), screening)


def z_rows(block):
    z, yl = divmod(block, 2)
    return slice(4 * z, 4 * z + 4), yl


def solve_z_kernel(x_ref, eh, el, oh, ol, inverse_ref, out_ref, scaled):
    flipper = mirror()
    sym, anti = [], []
    for block in range(4):
        low = x_ref[z_rows(block)].reshape(TILE, TILE)
        high = x_ref[z_rows(7 - block)].reshape(TILE, TILE)
        high = flip_rows(high, flipper)
        sym.append(split(low + high))
        anti.append(split(low - high))
    for parity, sides, matrix in ((0, sym, (eh, el)), (1, anti, (oh, ol))):
        right = tuple(jnp.concatenate([s[i] for s in sides], 0) for i in range(2))
        for block in range(4):
            part = slice(block * TILE, (block + 1) * TILE)
            spectral = product((matrix[0][:, part], matrix[1][:, part]), right, TN)
            pair = split(spectral * inverse_ref[parity, part])
            scaled[parity, 0, part], scaled[parity, 1, part] = pair
    for block in range(4):
        rows = slice(block * TILE, (block + 1) * TILE)
        even = product((eh[rows], el[rows]), (scaled[0, 0], scaled[0, 1]), NN)
        odd = product((oh[rows], ol[rows]), (scaled[1, 0], scaled[1, 1]), NN)
        out_ref[z_rows(block)] = (even + odd).reshape(4, 64, TILE)
        flipped = flip_rows(even - odd, flipper)
        out_ref[z_rows(7 - block)] = flipped.reshape(4, 64, TILE)


def solve_z(x, matrices, weights):
    return call(
        solve_z_kernel,
        "solve_z",
        [VMEM] * 6,
        VMEM,
        jax.ShapeDtypeStruct((16, 2, 64, TILE), F32),
        [pltpu.VMEM((2, 2, HALF, TILE), BF16)],
        KERNEL_LIMIT,
        6 << 30,
    )(x, *matrices, weights)


def backward_y_kernel(across, x_ref, eh, el, oh, ol, near_ref, far_ref, halves):
    flipper = mirror()
    sides = []
    for parity in range(2):
        blocks = [x_ref[:, 4 * parity + i].reshape(ROWS, TILE) for i in range(4)]
        sides.append(split(jnp.concatenate(blocks, 1)))
    start = 512 * low_quarter(across)

    def keep(side, part, value):
        lanes = slice(part * TILE, (part + 1) * TILE)
        for plane in range(2):
            for half in range(2):
                rows = 128 * plane + 64 * half
                target = slice(64 * plane, 64 * plane + 64)
                halves[side, half, target, lanes] = value[rows : rows + 64]

    for part in range(2):
        rows = pl.ds(pl.multiple_of(start + part * TILE, TILE), TILE)
        even = product(sides[0], (eh[rows], el[rows]), NT)
        odd = product(sides[1], (oh[rows], ol[rows]), NT)
        keep(0, part, even + odd)
        keep(1, 1 - part, flip_lanes(even - odd, flipper))
    yh, yl = lax.axis_index("yh"), lax.axis_index("yl")
    for side, ref in ((yh, near_ref), (1 - yh, far_ref)):
        ref[0:128] = halves[side, yl]
        ref[128:256] = halves[side, 1 - yl]


def backward_y(across, x, matrices):
    def kernel(*refs):
        backward_y_kernel(across, *refs)

    return call(
        kernel,
        "backward_y",
        [VMEM] * 5,
        [VMEM] * 2,
        [jax.ShapeDtypeStruct((ROWS, 512), F32)] * 2,
        [pltpu.VMEM((2, 2, 128, 512), F32)],
        KERNEL_LIMIT,
        2 << 30,
    )(x, *matrices)


def place_kernel(where, *refs):
    out, sems = refs[-2], refs[-1]
    me, yl = lax.axis_index(NARROW), lax.axis_index("yl")

    def copy(index):
        d, half, array, row = where[index]
        start = ROWS * jnp.bitwise_xor(me, d) + 128 * jnp.bitwise_xor(yl, half)
        target = out.at[pl.ds(pl.multiple_of(start, 128), 128)]
        source = refs[array].at[pl.ds(row, 128)]
        return pltpu.make_async_copy(source, target, sems.at[index])

    for index in range(len(where)):
        copy(index).start()
    for index in range(len(where)):
        copy(index).wait()


def place(where, blocks, held):
    def kernel(*refs):
        place_kernel(where, *refs)

    more = [] if held is None else [held]
    return call(
        kernel,
        "place",
        [pl.BlockSpec(memory_space=pl.ANY)] * len(blocks) + [HBM] * len(more),
        HBM,
        jax.ShapeDtypeStruct((HALF, 512), F32),
        [pltpu.SemaphoreType.DMA((len(where),))],
        2,
        1 << 20,
        input_output_aliases={} if held is None else {len(blocks): 0},
    )(*blocks, *more)


def on_device(residual, counts, screening, even_y, odd_y, even_z, odd_z, lam_y, lam_z):
    block3, block2 = make_source((3, 2), residual, counts)
    block1, block0 = make_source((1, 0), residual, counts)
    block3, block1 = send(block3, 2), send(block1, 2)
    ways = [
        jnp.concatenate([block0[128:], block1[128:]]),
        jnp.concatenate([block2[:128], block3[:128]]),
        jnp.concatenate([block2[128:], block3[128:]]),
    ]
    first = [send(way, d, (0,)) for way, d in zip(ways, (1, 4, 5))]
    matrix_y, matrix_z = prepare(even_y, odd_y), prepare(even_z, odd_z)
    weights = inverse(lam_z, lam_y, screening)
    first, block1 = lax.optimization_barrier((first, block1))
    token = send(first[1][:8, :LANES], 2, (0,))
    ways, token = lax.optimization_barrier((ways, token))
    second = [send(way, d, (1,)) for way, d in zip(ways, (1, 4, 5))]
    block0, block1, matrix_y, matrix_z, weights = lax.optimization_barrier(
        (block0, block1, matrix_y, matrix_z, weights)
    )
    along = forward_y(1, block1, first, second, matrix_y, token, None)
    along = forward_y(0, block0, first, second, matrix_y, token, along)
    columns = lax.all_to_all(along.reshape(16, 2, 64, TILE), WIDE, 0, 0, tiled=True)
    back = solve_z(columns, matrix_z, weights)
    rows = lax.all_to_all(back, WIDE, 0, 0, tiled=True).reshape(2, 8, 2, 64, TILE)
    block1, block2 = backward_y(1, rows, matrix_y)
    block0, block3 = backward_y(0, rows, matrix_y)
    far = send(jnp.concatenate([block2[:128], block3[:128]]), 4)
    across = send(jnp.concatenate([block2[128:], block3[128:]]), 5)
    near = send(jnp.concatenate([block0[128:], block1[128:]]), 1)
    early, far, near = lax.optimization_barrier((block1[:128], far, near))
    early = send(jnp.concatenate([early, near[128:], far[128:]]), 2)
    late = send(across[128:], 2)
    out = place(
        ((0, 0, 0, 0), (0, 1, 1, 0), (2, 0, 2, 0), (2, 1, 3, 0)),
        (block0, near, far, across),
        None,
    )
    where = ((1, 0, 0, 0), (1, 1, 0, 128), (3, 0, 0, 256), (3, 1, 1, 0))
    out = place(where, (early, late), out)
    return out.reshape(16, 64, 512)


def solution(mesh):
    fine = Mesh(mesh.devices.reshape(2, 2, 4, 2, 4), ("yh", "core", "z", "yl", "x"))
    split_spec = P(None, ("z", "yl", "x"), NARROW)
    return jax.shard_map(
        on_device,
        mesh=fine,
        in_specs=(split_spec, split_spec) + (P(),) * 7,
        out_specs=split_spec,
        check_vma=False,
    )
```

```python
import jax
import jax.numpy as jnp
from jax import lax
from jax.experimental import pallas as pl
from jax.experimental.pallas import tpu as pltpu
from jax.sharding import Mesh, PartitionSpec as P

F32 = jnp.float32
BF16 = jnp.bfloat16
TILE = 256
LANES = 128
HALF = 1024
ROWS = 256
SOURCE_LIMIT = 52
PREPARE_LIMIT = 8
KERNEL_LIMIT = 12
NARROW = ("yh", "core")
WIDE = ("z", "yl", "x")
VMEM = pl.BlockSpec(memory_space=pltpu.VMEM)
HBM = pl.BlockSpec(memory_space=pltpu.HBM)
NN = (((1,), (0,)), ((), ()))
NT = (((1,), (1,)), ((), ()))
TN = (((0,), (0,)), ((), ()))


def split(value):
    high = value.astype(BF16)
    low = (value - high.astype(F32)).astype(BF16)
    return high, low


def dot(left, right, dims):
    return lax.dot_general(left, right, dims, preferred_element_type=F32)


def product(left, right, dims):
    return (
        dot(left[0], right[0], dims)
        + dot(left[0], right[1], dims)
        + dot(left[1], right[0], dims)
    )


def mirror():
    row = lax.broadcasted_iota(jnp.int32, (TILE, TILE), 0)
    column = lax.broadcasted_iota(jnp.int32, (TILE, TILE), 1)
    return jnp.where(row + column == TILE - 1, 1.0, 0.0).astype(BF16)


def flip_lanes(value, flipper):
    high, low = split(value)
    return dot(high, flipper, NN) + dot(low, flipper, NN)


def flip_rows(value, flipper):
    high, low = split(value)
    return dot(flipper, high, NN) + dot(flipper, low, NN)


def low_quarter(across):
    core, yh = lax.axis_index("core"), lax.axis_index("yh")
    return jnp.bitwise_xor(jnp.bitwise_xor(core, yh), across)


def call(kernel, name, in_specs, out_specs, out_shape, scratch, limit, flops, **more):
    return pl.pallas_call(
        kernel,
        in_specs=in_specs,
        out_specs=out_specs,
        out_shape=out_shape,
        scratch_shapes=scratch,
        compiler_params=pltpu.CompilerParams(vmem_limit_bytes=limit << 20),
        cost_estimate=pl.CostEstimate(flops=flops, transcendentals=0, bytes_accessed=10 << 20),
        name=name,
        **more,
    )


def source_kernel(order, residual, counts, *refs):
    outs, residual_buffer, counts_buffer, sems = refs[:-3], *refs[-3:]
    me = lax.axis_index(NARROW)
    steps = [(i, part) for i in range(len(order)) for part in range(2)]

    def copies(step):
        i, part = step
        planes = pl.ds(4 * jnp.bitwise_xor(me, order[i]) + 2 * part, 2)
        slot = 2 * i + part
        yield pltpu.make_async_copy(residual.at[planes], residual_buffer.at[slot], sems.at[0, slot])
        yield pltpu.make_async_copy(counts.at[planes], counts_buffer.at[slot], sems.at[1, slot])

    for step in steps:
        for copy in copies(step):
            copy.start()
    for step in steps:
        for copy in copies(step):
            copy.wait()
        i, part = step
        slot = 2 * i + part
        value = residual_buffer[slot] + 0.3 * (counts_buffer[slot].astype(F32) - 2.0)
        outs[i][part * 128 : (part + 1) * 128] = value.reshape(128, 512)


def make_source(order, residual, counts):
    def kernel(*refs):
        source_kernel(order, *refs)

    count = len(order)
    return call(
        kernel,
        "make_source",
        [HBM] * 2,
        [VMEM] * count,
        [jax.ShapeDtypeStruct((ROWS, 512), F32)] * count,
        [
            pltpu.VMEM((2 * count, 2, 64, 512), F32),
            pltpu.VMEM((2 * count, 2, 64, 512), jnp.int32),
            pltpu.SemaphoreType.DMA((2, 2 * count)),
        ],
        SOURCE_LIMIT,
        1 << 20,
    )(residual, counts)


def prepare_kernel(*refs):
    matrices, outs, buffer, sems = refs[:2], refs[2:6], *refs[6:]
    steps = [(m, r) for m in range(2) for r in range(4)]

    def fetch(index):
        matrix, rows = steps[index]
        source = matrices[matrix].at[pl.ds(rows * TILE, TILE)]
        return pltpu.make_async_copy(source, buffer.at[index % 4], sems.at[index % 4])

    for index in range(3):
        fetch(index).start()
    for index, (matrix, rows) in enumerate(steps):
        if index + 3 < 8:
            fetch(index + 3).start()
        fetch(index).wait()
        high, low = split(buffer[index % 4])
        outs[2 * matrix][rows * TILE : (rows + 1) * TILE] = high
        outs[2 * matrix + 1][rows * TILE : (rows + 1) * TILE] = low


def prepare(*matrices):
    return call(
        prepare_kernel,
        "prepare",
        [HBM] * 2,
        [VMEM] * 4,
        [jax.ShapeDtypeStruct((HALF, HALF), BF16)] * 4,
        [pltpu.VMEM((4, TILE, HALF), F32), pltpu.SemaphoreType.DMA((4,))],
        PREPARE_LIMIT,
        2 << 30,
    )(*matrices)


def send(block, d, cores=(0, 1)):
    return lax.ppermute(block, NARROW, [(n, n ^ d) for n in range(4) if n % 2 in cores])


def forward_y_kernel(across, near_ref, far0_ref, far1_ref, eh, el, oh, ol, _, *refs):
    held, out_ref, halves = refs[:-2], refs[-2], refs[-1]
    yh = lax.axis_index("yh")
    halves[yh] = near_ref[...]
    for core, far_ref in enumerate((far0_ref, far1_ref)):

        @pl.when(lax.axis_index("core") == core)
        def _(far_ref=far_ref):
            halves[1 - yh] = far_ref[...]

    flipper = mirror()
    sym, anti = [], []
    for part in range(2):
        low = halves[0, :, part * TILE : (part + 1) * TILE]
        high = flip_lanes(halves[1, :, (1 - part) * TILE : (2 - part) * TILE], flipper)
        sym.append(split(low + high))
        anti.append(split(low - high))
    rows = pl.ds(pl.multiple_of(512 * low_quarter(across), 512), 512)
    for base, sides, high, low in ((0, sym, eh, el), (4, anti, oh, ol)):
        left = tuple(jnp.concatenate([s[i] for s in sides], 1) for i in range(2))
        for block in range(4):
            lanes = slice(block * TILE, (block + 1) * TILE)
            result = product(left, (high[rows, lanes], low[rows, lanes]), NN)
            result = result.reshape(4, 64, TILE)
            if held:
                result = result + held[0][:, base + block]
            out_ref[:, base + block] = result


def forward_y(across, near, far, matrices, token, held):
    def kernel(*refs):
        forward_y_kernel(across, *refs)

    more = [] if held is None else [held]
    return call(
        kernel,
        "forward_y",
        [VMEM] * (8 + len(more)),
        VMEM,
        jax.ShapeDtypeStruct((4, 8, 64, TILE), F32),
        [pltpu.VMEM((2, ROWS, 512), F32)],
        KERNEL_LIMIT,
        2 << 30,
    )(near, *far, *matrices, token, *more)


def pieces(value):
    high = value.astype(BF16)
    rest = value - high.astype(F32)
    middle = rest.astype(BF16)
    low = (rest - middle.astype(F32)).astype(BF16)
    return [high.astype(F32), middle.astype(F32), low.astype(F32)]


def inverse_kernel(lamz_ref, lamy_ref, screen_ref, out_ref):
    place = lax.axis_index(WIDE)
    plane, modes = 4 * lax.axis_index(NARROW) + place // 8, place % 8
    shift = jnp.concatenate([lamy_ref[pl.ds(2 * modes + i, 1)] for i in range(2)], 1)
    shift = pieces(shift + screen_ref[plane])
    shift = jnp.concatenate(shift + [jnp.ones((1, TILE), F32)] * 3, 0).astype(BF16)
    for parity in range(2):
        lam = jnp.concatenate([lamz_ref[8 * parity + i : 8 * parity + i + 1] for i in range(8)], 1)
        lam = jnp.concatenate([jnp.ones((1, HALF), F32)] * 3 + pieces(lam), 0).astype(BF16)
        out_ref[parity] = 1.0 / dot(lam, shift, TN)


def inverse(lam_z, lam_y, screening):
    return call(
        inverse_kernel,
        "inverse",
        [VMEM] * 2 + [pl.BlockSpec(memory_space=pltpu.SMEM)],
        VMEM,
        jax.ShapeDtypeStruct((2, HALF, TILE), F32),
        [],
        8,
        1 << 30,
    )(lam_z.reshape(16, LANES), lam_y.reshape(16, LANES), screening)


def solve_z_kernel(x_ref, eh, el, oh, ol, inverse_ref, out_ref, scaled):
    flipper = mirror()
    sym, anti = [], []
    for block in range(4):
        low = x_ref[4 * block : 4 * block + 4].reshape(TILE, TILE)
        high = x_ref[28 - 4 * block : 32 - 4 * block].reshape(TILE, TILE)
        high = flip_rows(high, flipper)
        sym.append(split(low + high))
        anti.append(split(low - high))
    for parity, sides, matrix in ((0, sym, (eh, el)), (1, anti, (oh, ol))):
        right = tuple(jnp.concatenate([s[i] for s in sides], 0) for i in range(2))
        for block in range(4):
            part = slice(block * TILE, (block + 1) * TILE)
            spectral = product((matrix[0][:, part], matrix[1][:, part]), right, TN)
            pair = split(spectral * inverse_ref[parity, part])
            scaled[parity, 0, part], scaled[parity, 1, part] = pair
    for block in range(4):
        rows = slice(block * TILE, (block + 1) * TILE)
        even = product((eh[rows], el[rows]), (scaled[0, 0], scaled[0, 1]), NN)
        odd = product((oh[rows], ol[rows]), (scaled[1, 0], scaled[1, 1]), NN)
        out_ref[4 * block : 4 * block + 4] = (even + odd).reshape(4, 64, TILE)
        flipped = flip_rows(even - odd, flipper)
        out_ref[28 - 4 * block : 32 - 4 * block] = flipped.reshape(4, 64, TILE)


def solve_z(x, matrices, weights):
    return call(
        solve_z_kernel,
        "solve_z",
        [VMEM] * 6,
        VMEM,
        jax.ShapeDtypeStruct((32, 64, TILE), F32),
        [pltpu.VMEM((2, 2, HALF, TILE), BF16)],
        KERNEL_LIMIT,
        6 << 30,
    )(x, *matrices, weights)


def backward_y_kernel(across, x_ref, eh, el, oh, ol, near_ref, far_ref, halves):
    flipper = mirror()
    sides = []
    for parity in range(2):
        blocks = [x_ref[:, 4 * parity + i].reshape(ROWS, TILE) for i in range(4)]
        sides.append(split(jnp.concatenate(blocks, 1)))
    start = 512 * low_quarter(across)
    for part in range(2):
        rows = pl.ds(pl.multiple_of(start + part * TILE, TILE), TILE)
        even = product(sides[0], (eh[rows], el[rows]), NT)
        odd = product(sides[1], (oh[rows], ol[rows]), NT)
        halves[0, :, part * TILE : (part + 1) * TILE] = even + odd
        flipped = flip_lanes(even - odd, flipper)
        halves[1, :, (1 - part) * TILE : (2 - part) * TILE] = flipped
    yh = lax.axis_index("yh")
    near_ref[...] = halves[yh]
    far_ref[...] = halves[1 - yh]


def backward_y(across, x, matrices):
    def kernel(*refs):
        backward_y_kernel(across, *refs)

    return call(
        kernel,
        "backward_y",
        [VMEM] * 5,
        [VMEM] * 2,
        [jax.ShapeDtypeStruct((ROWS, 512), F32)] * 2,
        [pltpu.VMEM((2, ROWS, 512), F32)],
        KERNEL_LIMIT,
        2 << 30,
    )(x, *matrices)


def place_kernel(order, *refs):
    blocks, out, sems = refs[: len(order)], refs[-2], refs[-1]
    me = lax.axis_index(NARROW)
    steps = [(i, part) for i in range(len(order)) for part in range(2)]

    def copy(i, part):
        start = ROWS * jnp.bitwise_xor(me, order[i]) + part * 128
        target = out.at[pl.ds(pl.multiple_of(start, 128), 128)]
        source = blocks[i].at[pl.ds(part * 128, 128)]
        return pltpu.make_async_copy(source, target, sems.at[i, part])

    for step in steps:
        copy(*step).start()
    for step in steps:
        copy(*step).wait()


def place(order, blocks, held):
    def kernel(*refs):
        place_kernel(order, *refs)

    more = [] if held is None else [held]
    return call(
        kernel,
        "place",
        [pl.BlockSpec(memory_space=pl.ANY)] * len(order) + [HBM] * len(more),
        HBM,
        jax.ShapeDtypeStruct((HALF, 512), F32),
        [pltpu.SemaphoreType.DMA((len(order), 2))],
        2,
        1 << 20,
        input_output_aliases={} if held is None else {len(order): 0},
    )(*blocks, *more)


def on_device(residual, counts, screening, even_y, odd_y, even_z, odd_z, lam_y, lam_z):
    block3, block2 = make_source((3, 2), residual, counts)
    block1, block0 = make_source((1, 0), residual, counts)
    block3, block1, block0 = lax.optimization_barrier((send(block3, 1), block1, block0))
    own0, sibling0 = send(block2, 2, (0,)), send(block3, 2, (0,))
    block1 = send(block1, 1)
    matrix_y, matrix_z = prepare(even_y, odd_y), prepare(even_z, odd_z)
    weights = inverse(lam_z, lam_y, screening)
    block1, sibling0, own0, matrix_y, matrix_z, weights = lax.optimization_barrier(
        (block1, sibling0, own0, matrix_y, matrix_z, weights)
    )
    token = send(sibling0[:8, :LANES], 1, (0,))
    block2, block3, token = lax.optimization_barrier((block2, block3, token))
    own1, sibling1 = send(block2, 2, (1,)), send(block3, 2, (1,))
    along = forward_y(1, block1, (own0, own1), matrix_y, token, None)
    along = forward_y(0, block0, (sibling0, sibling1), matrix_y, token, along)
    columns = lax.all_to_all(along.reshape(32, 64, TILE), WIDE, 0, 0, tiled=True)
    back = solve_z(columns, matrix_z, weights)
    rows = lax.all_to_all(back, WIDE, 0, 0, tiled=True).reshape(4, 8, 64, TILE)
    block1, block2 = backward_y(1, rows, matrix_y)
    block0, block3 = backward_y(0, rows, matrix_y)
    block2, block3 = send(block2, 2), send(block3, 2)
    block1, block2 = lax.optimization_barrier((block1, block2))
    block1, block3 = send(block1, 1), send(block3, 1)
    out = place((0, 1, 2), (block0, block1, block2), None)
    out = place((3,), (block3,), out)
    return out.reshape(16, 64, 512)


def solution(mesh):
    fine = Mesh(mesh.devices.reshape(2, 2, 4, 2, 4), ("yh", "core", "z", "yl", "x"))
    split_spec = P(None, WIDE, NARROW)
    return jax.shard_map(
        on_device,
        mesh=fine,
        in_specs=(split_spec, split_spec) + (P(),) * 7,
        out_specs=split_spec,
        check_vma=False,
    )
```
